32 devices in a mesh: groups: 2 (over x), tensor: 16 (over z, y, core).
Axes of the slice: x: 2, y: 2, z: 4, core: 2. Of those that a mesh axis runs over, the one named last changes fastest.
Arguments:
- queries: bfloat16 [16, 16384], P('groups', 'tensor'), parts along dimension 0, may hold values from -120 to 120
- kv_cache: bfloat16 [2, 16, 512, 1024], P(None, 'groups', 'tensor'), parts along dimension 1, may hold values from -4 to 4
- lengths: int32 [16], P('groups'), parts along dimension 0, may hold values from 2 to 512, as said below
- out_weight: bfloat16 [16384, 16384], P('tensor'), may hold values from -0.8984375 to 0.8984375
- outlier_values: bfloat16 [128, 4, 128, 128], P('tensor'), may hold values from -3 to 3
- outlier_columns: int32 [128, 4], P('tensor'), may hold values from 0 to 127
- outlier_counts: int32 [128], P('tensor'), may hold values from 1 to 4, as said below
Outputs:
- mixed: bfloat16 [16, 16384], P('groups', 'tensor'), parts along dimension 0
The draws below stay inside these ranges and needn't reach their ends.
There are 2 independent parts, one for each index of `groups`. The reference program is written for one: setup_inputs(seed, part) draws one part's arguments, and reference() takes and returns one part's arrays. A program takes and returns all parts, laid end to end along the dimension named above; an argument that names none is the same for every part. Nothing has to cross between parts.
Inputs may be any that keep to these rules, and one draw needn't show every extreme that they name: `lengths`: some request has all 512 positions live and some has 2. `outlier_counts`: some head has all 4 slots live and some has one.
All inputs are finite; a program needn't handle non-finite values.
Results may differ from the reference program's by a relative error of at most 0.0057.
Values may be sent and summed in bfloat16 or wider, within the bound.
A program may use at most 128 MiB of HBM per device.

```python
import math
import jax
import jax.numpy as jnp
from jax import lax

D = 16384
HEADS = 128
KVH = 8
HD = 128
OBLK = 128
OMAX = 4
ROWS = 8
SEQ = 512


def attention_pair(key):
    folded = jax.random.fold_in(key, 7)
    query_key, cache_key = jax.random.split(folded, 2)
    cache_drawn = jnp.clip(jax.random.normal(cache_key, (2, ROWS, SEQ, KVH * HD), jnp.float32), -4.0, 4.0)
    query_drawn = jnp.clip(jax.random.normal(query_key, (ROWS, HEADS * HD), jnp.float32), -4.0, 4.0)
    return (query_drawn, cache_drawn)


def draw_queries(key, part):
    return attention_pair(key)[0].astype(jnp.bfloat16)


def draw_kv_cache(key, part):
    return attention_pair(key)[1].astype(jnp.bfloat16)


def draw_lengths(key, part):
    folded = jax.random.fold_in(key, 11)
    key_one, key_two, key_three = jax.random.split(folded, 3)
    drawn = jax.random.randint(key_one, (ROWS,), 2, SEQ + 1, dtype=jnp.int32)
    first_row = jax.random.randint(key_two, (), 0, ROWS, dtype=jnp.int32)
    second_row = (first_row + 1 + jax.random.randint(key_three, (), 0, ROWS - 1, dtype=jnp.int32)) % ROWS
    return drawn.at[first_row].set(SEQ).at[second_row].set(2)


def draw_outlier_counts(key, part):
    folded = jax.random.fold_in(key, 13)
    key_one, key_two, key_three = jax.random.split(folded, 3)
    drawn = jax.random.randint(key_one, (HEADS,), 1, OMAX + 1, dtype=jnp.int32)
    first_head = jax.random.randint(key_two, (), 0, HEADS, dtype=jnp.int32)
    second_head = (first_head + 1 + jax.random.randint(key_three, (), 0, HEADS - 1, dtype=jnp.int32)) % HEADS
    return drawn.at[first_head].set(OMAX).at[second_head].set(1)


def touch_ends(values, stream_key, least, high):
    extent = values.shape
    place = [jax.random.randint(jax.random.fold_in(stream_key, axis), (), 0, extent[axis]) for axis in range(len(extent))]
    values = values.at[tuple(place)].set(least)
    longest = extent.index(max(extent))
    place[longest] = (place[longest] + 1) % extent[longest]
    return values.at[tuple(place)].set(high)


def with_spikes(entries, key, source, target, shards_of, factor):
    owner, partner = [(jnp.arange(entries.shape[position]) // (entries.shape[position] // shards_of)).reshape([-1 if axis == position else 1 for axis in range(entries.ndim)]) for position in (source, target)]
    chosen = jax.random.permutation(key, shards_of)[partner]
    strong = (owner == chosen) | (owner == (partner + shards_of // 2) % shards_of)
    return jnp.where(strong, factor * entries, entries)


def shard_levels(rng, dims, pieces, least, top_value):
    level = 1.0
    for axis_at, parts in pieces:
        steps = jax.random.uniform(jax.random.fold_in(jax.random.fold_in(rng, 6), axis_at), (parts,), jnp.float32, least / len(pieces), top_value / len(pieces))
        level = level * jnp.repeat(jnp.exp(steps), dims[axis_at] // parts).reshape((-1,) + (1,) * (len(dims) - 1 - axis_at))
    return level


def scatter_about(stream_key, extent, spread, reach, cuts=(), kind=jnp.bfloat16):
    gain = shard_levels(stream_key, extent, cuts, -0.22, 0.18) if cuts else 1.0
    values = jax.random.normal(stream_key, extent, jnp.float32) * spread * gain
    return jnp.minimum(jnp.maximum(values, -reach), reach).astype(kind)


def heavy_noise(own_key, dims, deviation, limit, shards, heavy, held_as=jnp.bfloat16):
    array = deviation * jax.random.normal(own_key, dims, jnp.float32)
    if shards:
        array = array * shard_levels(own_key, dims, shards, -0.22, 0.18)
    return jnp.clip(with_spikes(array, jax.random.fold_in(own_key, 3), *heavy), -limit, limit).astype(held_as)


def setup_inputs(seed: int = 0, part: int = 0) -> dict:
    arg_keys = jax.random.split(jax.random.key(seed), 8)
    part_keys = jax.random.split(jax.random.fold_in(arg_keys[7], part), 8)
    return {
        "queries": draw_queries(jax.random.fold_in(jax.random.fold_in(arg_keys[7], part), 71), part),
        "kv_cache": draw_kv_cache(jax.random.fold_in(jax.random.fold_in(arg_keys[7], part), 71), part),
        "lengths": draw_lengths(jax.random.fold_in(jax.random.fold_in(arg_keys[7], part), 71), part),
        "out_weight": heavy_noise(arg_keys[3], (HEADS * HD, D), 0.15, 0.8984375, ((0, 16),), (0, 1, 16, 2.0)),
        "outlier_values": scatter_about(arg_keys[4], (HEADS, OMAX, HD, OBLK), 0.5, 3.0, ((0, 16),)),
        "outlier_columns": touch_ends(jax.random.randint(arg_keys[5], (HEADS, OMAX), 0, D // OBLK), jax.random.fold_in(arg_keys[5], 1), 0, (D // OBLK) - 1).astype(jnp.int32),
        "outlier_counts": draw_outlier_counts(jax.random.fold_in(arg_keys[7], 71), part),
    }


def reference(queries, kv_cache, lengths, out_weight, outlier_values, outlier_columns, outlier_counts):
    row_count = queries.shape[0]
    group_size = HEADS // KVH
    key_rows = kv_cache[0].reshape(row_count, SEQ, KVH, HD).astype(jnp.float32)
    value_rows = kv_cache[1].reshape(row_count, SEQ, KVH, HD).astype(jnp.float32)
    queried = queries.reshape(row_count, KVH, group_size, HD).astype(jnp.float32)
    scores = jnp.einsum('rkgd,rskd->rkgs', queried, key_rows) / math.sqrt(HD)
    visible = jnp.arange(SEQ, dtype=jnp.int32)[None, :] < lengths[:, None]
    scores = jnp.where(visible[:, None, None, :], scores, -1e+30)
    row_peak = lax.optimization_barrier(jnp.max(scores, axis=-1, keepdims=True))
    raised = jnp.exp(scores - row_peak)
    totals = lax.optimization_barrier(jnp.sum(raised, axis=-1, keepdims=True))
    weights = (raised / totals).astype(jnp.bfloat16)
    attended = jnp.einsum('rkgs,rskd->rkgd', weights.astype(jnp.float32), value_rows)
    attended = attended.reshape(row_count, HEADS * HD).astype(jnp.bfloat16)
    projected = jnp.dot(attended, out_weight, preferred_element_type=jnp.float32)
    heads_attended = attended.reshape(row_count, HEADS, HD).astype(jnp.float32)
    slot_live = jnp.arange(OMAX, dtype=jnp.int32)[None, :] < outlier_counts[:, None]
    outlier_terms = jnp.einsum('rhd,hodc->rhoc', heads_attended, outlier_values.astype(jnp.float32))
    placement = ((outlier_columns[:, :, None] == jnp.arange(D // OBLK, dtype=jnp.int32)[None, None, :]) & slot_live[:, :, None]).astype(jnp.float32)
    correction = jnp.einsum('rhoc,hob->rbc', outlier_terms, placement).reshape(row_count, D)
    return (projected + correction).astype(jnp.bfloat16)
```

```python
import functools
import math

import jax
import jax.numpy as jnp
from jax import lax
from jax.experimental import pallas as pl
from jax.experimental.pallas import tpu as pltpu
from jax.sharding import PartitionSpec as P

KVH = 8
HD = 128
STAT = 16
MESH = pl.DeviceIdType.MESH
F32 = jnp.float32
BF16 = jnp.bfloat16


def flip(a, b, n):
    out, bit = 0, 1
    while bit < n:
        out = out + ((a // bit + b // bit) % 2) * bit
        bit *= 2
    return out


def kernel(
    n,
    q_hbm, kv_hbm, w_hbm, ov_hbm, len_ref, col_ref, cnt_ref,
    out_ref,
    qbuf, kvbuf, wbuf, ovbuf, bias, osend, obuf, abuf, tbuf, sbuf, rbuf,
    kv_sem, kvs_sem, kvr_sem, qs_sem, qr_sem, w_sem, ov_sem, os_sem, or_sem, ss_sem, sr_sem,
):
    me = lax.axis_index("tensor")
    core = me % 2
    chip = me // 2
    partner = me + 1 - 2 * core
    chips = n // 2
    half = me // chips
    rows, width = q_hbm.shape
    hl = width // HD
    nr = hl * rows
    g = n // KVH
    kh = KVH // 2
    positions = kv_hbm.shape[2]
    cols = w_hbm.shape[1] // n
    omax = ov_hbm.shape[1]
    jb = cols // HD
    hw = kh * HD
    kvcols = rows * positions

    def kv_half(c):
        return kv_hbm.at[:, :, :, pl.ds(pl.multiple_of(c * hw, hw), hw)]

    kv_own = pltpu.make_async_copy(kv_half(core), kvbuf.at[0], kv_sem)
    kv_own.start()
    ov_copy = pltpu.make_async_copy(ov_hbm, ovbuf, ov_sem)
    my_slot = me - half * chips

    barrier = pltpu.get_barrier_semaphore()

    @pl.loop(1, n)
    def _(i):
        pl.semaphore_signal(barrier, inc=1, device_id={"tensor": flip(me, i, n)}, device_id_type=MESH)

    @pl.when(half == core)
    def _():
        pltpu.make_async_copy(q_hbm, qbuf.at[my_slot], qr_sem.at[my_slot]).start()

    def w_copy(i):
        dest = flip(me, n - 1 - i, n)
        return pltpu.make_async_copy(
            w_hbm.at[:, pl.ds(pl.multiple_of(dest * cols, cols), cols)], wbuf.at[i], w_sem.at[i]
        )

    rowreq = lax.broadcasted_iota(jnp.int32, (g * nr, kvcols), 0) % rows
    colidx = lax.broadcasted_iota(jnp.int32, (1, kvcols), 1)
    colreq = colidx // positions
    limit = jnp.zeros((1, kvcols), jnp.int32)
    for r in range(rows):
        limit = jnp.where(colreq == r, len_ref[r], limit)
    for part in range(2):
        dev = me if part == 0 else partner
        live = (colidx % positions + dev * positions) < limit
        tag = jnp.where(live, colreq, -1)
        bias[part] = jnp.where(rowreq == tag, 0.0, -1e30).astype(F32)

    pl.semaphore_wait(barrier, n - 1)

    swap = pltpu.make_async_remote_copy(
        src_ref=kv_half(1 - core), dst_ref=kvbuf.at[1], send_sem=kvs_sem, recv_sem=kvr_sem,
        device_id={"tensor": partner}, device_id_type=MESH,
    )
    swap.start()

    def q_send(i):
        p = flip(chip, chips - 1 - i, chips)
        target = 2 * p + half
        return target, pltpu.make_async_remote_copy(
            src_ref=q_hbm, dst_ref=qbuf.at[my_slot], send_sem=qs_sem.at[i], recv_sem=qr_sem.at[my_slot],
            device_id={"tensor": target}, device_id_type=MESH,
        )

    @pl.loop(0, chips)
    def _(i):
        target, copy = q_send(i)

        @pl.when(target != me)
        def _():
            copy.start()

    @pl.loop(0, n)
    def _(i):
        w_copy(i).start()

    ov_copy.start()

    kv_own.wait()
    swap.wait()

    eye = lax.broadcasted_iota(jnp.int32, (g * nr, HD), 0) == lax.broadcasted_iota(jnp.int32, (g * nr, HD), 1)
    stat_row = lax.broadcasted_iota(jnp.int32, (STAT, HD), 0)

    def to_row(column):
        return jnp.sum(jnp.where(eye, column, 0.0), axis=0, keepdims=True)

    def o_send(j):
        target = core * chips + j
        return target, pltpu.make_async_remote_copy(
            src_ref=osend.at[j], dst_ref=obuf.at[chip], send_sem=os_sem.at[j], recv_sem=or_sem.at[chip],
            device_id={"tensor": target}, device_id_type=MESH,
        )

    def o_local(j):
        return pltpu.make_async_copy(osend.at[j], obuf.at[chip], or_sem.at[chip])

    for kl in range(kh):
        pieces = []
        for dl in range(g):
            slot = kl * g + dl
            pltpu.make_async_copy(qbuf.at[slot], qbuf.at[slot], qr_sem.at[slot]).wait()
            got = qbuf[slot].astype(F32)
            pieces += [got[:, h * HD:(h + 1) * HD] for h in range(hl)]
        q = jnp.concatenate(pieces, axis=0).astype(BF16)
        scores, values = [], []
        for part in range(2):
            keys = kvbuf[part, 0, :, :, kl * HD:(kl + 1) * HD].reshape(kvcols, HD)
            values.append(kvbuf[part, 1, :, :, kl * HD:(kl + 1) * HD].reshape(kvcols, HD))
            s = lax.dot_general(q, keys, (((1,), (1,)), ((), ())), preferred_element_type=F32)
            scores.append(s * (1.0 / math.sqrt(HD)) + bias[part])
        peak = jnp.maximum(
            jnp.max(scores[0], axis=-1, keepdims=True), jnp.max(scores[1], axis=-1, keepdims=True)
        )
        peak = jnp.maximum(peak, -(2.0**66)).astype(BF16).astype(F32)
        total = jnp.zeros((g * nr, 1), F32)
        o = jnp.zeros((g * nr, HD), F32)
        for part in range(2):
            raised = jnp.exp(scores[part] - peak)
            total = total + jnp.sum(raised, axis=-1, keepdims=True)
            o = o + jnp.dot(raised.astype(BF16), values[part], preferred_element_type=F32)
        total_row = to_row(total)
        total_hi = total_row.astype(BF16).astype(F32)
        stats = jnp.where(
            stat_row == 0, to_row(peak), jnp.where(stat_row == 1, total_hi, total_row - total_hi)
        ).astype(BF16)
        o = o.astype(BF16)
        for dl in range(g):
            slot = kl * g + dl
            osend[slot, :nr, :] = o[dl * nr:(dl + 1) * nr]
            osend[slot, nr:, :] = stats
            target, copy = o_send(slot)

            @pl.when(target != me)
            def _():
                copy.start()

            @pl.when(target == me)
            def _():
                o_local(slot).start()

    for p in range(chips):
        pltpu.make_async_copy(obuf.at[p], obuf.at[p], or_sem.at[p]).wait()
    peaks, totals = [], []
    for p in range(chips):
        st = obuf[p, nr:, :].astype(F32)
        peaks.append(st[0:1])
        totals.append(st[1:2] + st[2:3])
    peak = functools.reduce(jnp.maximum, peaks)
    shares = [jnp.exp(m - peak) for m in peaks]
    total = sum(s * t for s, t in zip(shares, totals))
    first = (me % g) * nr
    mine = (
        lax.broadcasted_iota(jnp.int32, (nr, HD), 0) + first
        == lax.broadcasted_iota(jnp.int32, (nr, HD), 1)
    )
    attended = jnp.zeros((nr, HD), F32)
    for p in range(chips):
        share = jnp.sum(jnp.where(mine, shares[p] / total, 0.0), axis=1, keepdims=True)
        attended = attended + share * obuf[p, :nr, :].astype(F32)
    a = jnp.concatenate([attended[h * rows:(h + 1) * rows] for h in range(hl)], axis=1).astype(BF16)
    abuf[...] = a

    ov_copy.wait()
    for h in range(hl):
        for o in range(omax):
            tbuf[h * omax + o] = jnp.dot(
                a[:, h * HD:(h + 1) * HD], ovbuf[h, o], preferred_element_type=F32
            )

    def block(i):
        dest = flip(me, n - 1 - i, n)
        w_copy(i).wait()
        part = jnp.dot(abuf[...], wbuf[i], preferred_element_type=F32)
        sums = [part[:, j * HD:(j + 1) * HD] for j in range(jb)]
        for h in range(hl):
            for o in range(omax):
                col = jnp.where(o < cnt_ref[h], col_ref[h, o] - dest * jb, -1)
                colv = jnp.full((rows, HD), col, jnp.int32)
                term = tbuf[h * omax + o]
                sums = [s + jnp.where(colv == j, term, 0.0) for j, s in enumerate(sums)]
        return dest, jnp.concatenate(sums, axis=1)

    def s_send(i, dest):
        return pltpu.make_async_remote_copy(
            src_ref=sbuf.at[i], dst_ref=rbuf.at[i], send_sem=ss_sem.at[i], recv_sem=sr_sem.at[i],
            device_id={"tensor": dest}, device_id_type=MESH,
        )

    @pl.loop(0, n - 1)
    def _(i):
        dest, sums = block(i)
        sbuf[i] = sums.astype(sbuf.dtype)
        s_send(i, dest).start()

    _, acc = block(n - 1)


    @pl.loop(0, chips)
    def _(i):
        target, copy = q_send(i)

        @pl.when(target != me)
        def _():
            copy.wait_send()

        target2, copy2 = o_send(i)

        @pl.when(target2 != me)
        def _():
            copy2.wait_send()

    def gather(i, acc):
        dest = flip(me, n - 1 - i, n)
        s_send(i, dest).wait()
        return acc + rbuf[i].astype(F32)

    out_ref[...] = lax.fori_loop(0, n - 1, gather, acc)


def body(n, queries, kv_cache, lengths, out_weight, outlier_values, outlier_columns, outlier_counts):
    rows, width = queries.shape
    hl = width // HD
    nr = hl * rows
    positions = kv_cache.shape[2]
    cols = out_weight.shape[1] // n
    omax = outlier_values.shape[1]
    chips = n // 2
    g = n // KVH
    dma = pltpu.SemaphoreType.DMA
    out = pl.pallas_call(
        functools.partial(kernel, n),
        out_shape=jax.ShapeDtypeStruct((rows, cols), F32),
        in_specs=[pl.BlockSpec(memory_space=pl.ANY)] * 4 + [pl.BlockSpec(memory_space=pltpu.SMEM)] * 3,
        out_specs=pl.BlockSpec(memory_space=pltpu.VMEM),
        scratch_shapes=[
            pltpu.VMEM((chips, rows, width), BF16),
            pltpu.VMEM((2, 2, rows, positions, KVH // 2 * HD), BF16),
            pltpu.VMEM((n, width, cols), BF16),
            pltpu.VMEM(outlier_values.shape, BF16),
            pltpu.VMEM((2, g * nr, rows * positions), F32),
            pltpu.VMEM((chips, nr + STAT, HD), BF16),
            pltpu.VMEM((chips, nr + STAT, HD), BF16),
            pltpu.VMEM((rows, width), BF16),
            pltpu.VMEM((hl * omax, rows, HD), F32),
            pltpu.VMEM((n, rows, cols), BF16),
            pltpu.VMEM((n, rows, cols), BF16),
            dma, dma, dma, dma((chips,)), dma((chips,)), dma((n,)), dma, dma((chips,)), dma((chips,)),
            dma((n,)), dma((n,)),
        ],
        compiler_params=pltpu.CompilerParams(
            collective_id=0, has_side_effects=True, vmem_limit_bytes=60 * 2**20
        ),
    )(queries, kv_cache, out_weight, outlier_values, lengths, outlier_columns, outlier_counts)
    return out.astype(BF16)


def solution(mesh):
    placed = (
        P("groups", "tensor"),
        P(None, "groups", "tensor", None),
        P("groups"),
        P("tensor", None),
        P("tensor", None, None, None),
        P("tensor", None),
        P("tensor"),
    )
    return jax.shard_map(
        functools.partial(body, mesh.shape["tensor"]),
        mesh=mesh, in_specs=placed, out_specs=P("groups", "tensor"), check_vma=False,
    )
```

```python
import functools
import math

import jax
import jax.numpy as jnp
from jax import lax
from jax.experimental import pallas as pl
from jax.experimental.pallas import tpu as pltpu
from jax.sharding import PartitionSpec as P

KVH = 8
HD = 128
STAT = 16
MESH = pl.DeviceIdType.MESH
F32 = jnp.float32
BF16 = jnp.bfloat16


def flip(a, b, n):
    out, bit = 0, 1
    while bit < n:
        out = out + ((a // bit + b // bit) % 2) * bit
        bit *= 2
    return out


def kernel(
    n,
    q_hbm, kv_hbm, w_hbm, ov_hbm, len_hbm, col_hbm, cnt_hbm,
    out_ref,
    len_ref, col_ref, cnt_ref, qbuf, kvbuf, wbuf, ovbuf, bias, osend, obuf, abuf, tbuf, psend, precv, sbuf, rbuf,
    small_sem, kv_sem, kvs_sem, kvr_sem, qs_sem, qr_sem, w_sem, ov_sem, os_sem, or_sem, ps_sem, pr_sem, ss_sem, sr_sem,
):
    me = lax.axis_index("tensor")
    core = me % 2
    chip = me // 2
    partner = me + 1 - 2 * core
    chips = n // 2
    half = me // chips
    rows, width = q_hbm.shape
    hl = width // HD
    nr = hl * rows
    g = n // KVH
    kh = KVH // 2
    positions = kv_hbm.shape[2]
    cols = w_hbm.shape[1] // n
    omax = ov_hbm.shape[1]
    jb = cols // HD
    hw = kh * HD
    kvcols = rows * positions

    barrier = pltpu.get_barrier_semaphore()
    for i in range(n - 1, 0, -1):
        pl.semaphore_signal(barrier, inc=1, device_id={"tensor": flip(me, i, n)}, device_id_type=MESH)

    def kv_half(c):
        return kv_hbm.at[:, :, :, pl.ds(pl.multiple_of(c * hw, hw), hw)]

    small = [
        pltpu.make_async_copy(src, dst, small_sem.at[i])
        for i, (src, dst) in enumerate(((len_hbm, len_ref), (col_hbm, col_ref), (cnt_hbm, cnt_ref)))
    ]
    for copy in small:
        copy.start()
    kv_own = pltpu.make_async_copy(kv_half(core), kvbuf.at[0], kv_sem)
    kv_own.start()
    ov_copy = pltpu.make_async_copy(ov_hbm, ovbuf, ov_sem)
    my_slot = me - half * chips

    @pl.when(half == core)
    def _():
        pltpu.make_async_copy(q_hbm, qbuf.at[my_slot], qr_sem.at[my_slot]).start()

    def w_copy(i):
        dest = 2 * flip(chip, chips - 1 - i // 2, chips) + (core + 1 + i % 2) % 2
        return pltpu.make_async_copy(
            w_hbm.at[:, pl.ds(pl.multiple_of(dest * cols, cols), cols)], wbuf.at[i], w_sem.at[i]
        )

    for copy in small:
        copy.wait()

    rowreq = lax.broadcasted_iota(jnp.int32, (g * nr, kvcols), 0) % rows
    colidx = lax.broadcasted_iota(jnp.int32, (1, kvcols), 1)
    colreq = colidx // positions
    limit = jnp.zeros((1, kvcols), jnp.int32)
    for r in range(rows):
        limit = jnp.where(colreq == r, len_ref[r], limit)
    for part in range(2):
        dev = me if part == 0 else partner
        live = (colidx % positions + dev * positions) < limit
        tag = jnp.where(live, colreq, -1)
        bias[part] = jnp.where(rowreq == tag, 0.0, -1e30).astype(F32)

    ov_copy.start()

    @pl.loop(0, n)
    def _(i):
        w_copy(i).start()

    pl.semaphore_wait(barrier, n - 1)

    swap = pltpu.make_async_remote_copy(
        src_ref=kv_half(1 - core), dst_ref=kvbuf.at[1], send_sem=kvs_sem, recv_sem=kvr_sem,
        device_id={"tensor": partner}, device_id_type=MESH,
    )
    swap.start()

    def q_send(i):
        p = flip(chip, chips - 1 - i, chips)
        target = 2 * p + half
        return target, pltpu.make_async_remote_copy(
            src_ref=q_hbm, dst_ref=qbuf.at[my_slot], send_sem=qs_sem.at[i], recv_sem=qr_sem.at[my_slot],
            device_id={"tensor": target}, device_id_type=MESH,
        )

    @pl.loop(0, chips)
    def _(i):
        target, copy = q_send(i)

        @pl.when(target != me)
        def _():
            copy.start()

    kv_own.wait()
    swap.wait()

    eye = lax.broadcasted_iota(jnp.int32, (g * nr, HD), 0) == lax.broadcasted_iota(jnp.int32, (g * nr, HD), 1)
    stat_row = lax.broadcasted_iota(jnp.int32, (STAT, HD), 0)

    def to_row(column):
        return jnp.sum(jnp.where(eye, column, 0.0), axis=0, keepdims=True)

    def o_send(j):
        target = core * chips + j
        return target, pltpu.make_async_remote_copy(
            src_ref=osend.at[j], dst_ref=obuf.at[chip], send_sem=os_sem.at[j], recv_sem=or_sem.at[chip],
            device_id={"tensor": target}, device_id_type=MESH,
        )

    def o_local(j):
        return pltpu.make_async_copy(osend.at[j], obuf.at[chip], or_sem.at[chip])

    upper = chip // (chips // 2)
    for step in range(kh):
        kl = step + upper * (kh - 1 - 2 * step)
        lanes = pl.ds(pl.multiple_of(kl * HD, HD), HD)
        pieces = []
        for dl in range(g):
            slot = kl * g + dl
            pltpu.make_async_copy(qbuf.at[slot], qbuf.at[slot], qr_sem.at[slot]).wait()
            got = qbuf[slot].astype(F32)
            pieces += [got[:, h * HD:(h + 1) * HD] for h in range(hl)]
        q = jnp.concatenate(pieces, axis=0).astype(BF16)
        scores, values = [], []
        for part in range(2):
            keys = kvbuf[part, 0, :, :, lanes].reshape(kvcols, HD)
            values.append(kvbuf[part, 1, :, :, lanes].reshape(kvcols, HD))
            s = lax.dot_general(q, keys, (((1,), (1,)), ((), ())), preferred_element_type=F32)
            scores.append(s * (1.0 / math.sqrt(HD)) + bias[part])
        peak = jnp.maximum(
            jnp.max(scores[0], axis=-1, keepdims=True), jnp.max(scores[1], axis=-1, keepdims=True)
        )
        peak = jnp.maximum(peak, -(2.0**66)).astype(BF16).astype(F32)
        total = jnp.zeros((g * nr, 1), F32)
        o = jnp.zeros((g * nr, HD), F32)
        for part in range(2):
            raised = jnp.exp(scores[part] - peak)
            total = total + jnp.sum(raised, axis=-1, keepdims=True)
            o = o + jnp.dot(raised.astype(BF16), values[part], preferred_element_type=F32)
        total_row = to_row(total)
        total_hi = total_row.astype(BF16).astype(F32)
        stats = jnp.where(
            stat_row == 0, to_row(peak), jnp.where(stat_row == 1, total_hi, total_row - total_hi)
        ).astype(BF16)
        o = o.astype(BF16)
        for dl in range(g):
            slot = kl * g + dl
            osend[slot, :nr, :] = o[dl * nr:(dl + 1) * nr]
            osend[slot, nr:, :] = stats
            target, copy = o_send(slot)

            @pl.when(target != me)
            def _():
                copy.start()

            @pl.when(target == me)
            def _():
                o_local(slot).start()

    for p in range(chips):
        pltpu.make_async_copy(obuf.at[p], obuf.at[p], or_sem.at[p]).wait()
    peaks, totals = [], []
    for p in range(chips):
        st = obuf[p, nr:, :].astype(F32)
        peaks.append(st[0:1])
        totals.append(st[1:2] + st[2:3])
    peak = functools.reduce(jnp.maximum, peaks)
    shares = [jnp.exp(m - peak) for m in peaks]
    total = sum(s * t for s, t in zip(shares, totals))
    first = (me % g) * nr
    mine = (
        lax.broadcasted_iota(jnp.int32, (nr, HD), 0) + first
        == lax.broadcasted_iota(jnp.int32, (nr, HD), 1)
    )
    attended = jnp.zeros((nr, HD), F32)
    for p in range(chips):
        share = jnp.sum(jnp.where(mine, shares[p] / total, 0.0), axis=1, keepdims=True)
        attended = attended + share * obuf[p, :nr, :].astype(F32)
    a = jnp.concatenate([attended[h * rows:(h + 1) * rows] for h in range(hl)], axis=1).astype(BF16)
    abuf[...] = a

    ov_copy.wait()
    for h in range(hl):
        for o in range(omax):
            tbuf[h * omax + o] = jnp.dot(
                a[:, h * HD:(h + 1) * HD], ovbuf[h, o], preferred_element_type=F32
            )

    def block(i):
        dest = 2 * flip(chip, chips - 1 - i // 2, chips) + (core + 1 + i % 2) % 2
        w_copy(i).wait()
        part = jnp.dot(abuf[...], wbuf[i], preferred_element_type=F32)
        sums = [part[:, j * HD:(j + 1) * HD] for j in range(jb)]
        for h in range(hl):
            for o in range(omax):
                col = jnp.where(o < cnt_ref[h], col_ref[o, h] - dest * jb, -1)
                colv = jnp.full((rows, HD), col, jnp.int32)
                term = tbuf[h * omax + o]
                sums = [s + jnp.where(colv == j, term, 0.0) for j, s in enumerate(sums)]
        return jnp.concatenate(sums, axis=1)

    def p_send(i):
        return pltpu.make_async_remote_copy(
            src_ref=psend.at[i], dst_ref=precv.at[i], send_sem=ps_sem.at[i], recv_sem=pr_sem.at[i],
            device_id={"tensor": partner}, device_id_type=MESH,
        )

    def s_send(i):
        return pltpu.make_async_remote_copy(
            src_ref=sbuf.at[i], dst_ref=rbuf.at[i], send_sem=ss_sem.at[i], recv_sem=sr_sem.at[i],
            device_id={"tensor": 2 * flip(chip, chips - 1 - i, chips) + core}, device_id_type=MESH,
        )

    psend[0] = block(0)
    p_send(0).start()

    @pl.loop(0, chips - 1)
    def _(i):
        psend[i + 1] = block(2 * i + 2)
        p_send(i + 1).start()
        sums = block(2 * i + 1)
        p_send(i).wait_recv()
        sbuf[i] = (sums + precv[i]).astype(sbuf.dtype)
        s_send(i).start()

    acc = block(n - 1)
    p_send(chips - 1).wait_recv()
    acc = acc + precv[chips - 1]

    @pl.loop(0, chips)
    def _(i):
        target, copy = q_send(i)

        @pl.when(target != me)
        def _():
            copy.wait_send()

        target2, copy2 = o_send(i)

        @pl.when(target2 != me)
        def _():
            copy2.wait_send()

        p_send(i).wait_send()

    def gather(i, acc):
        s_send(i).wait()
        return acc + rbuf[i].astype(F32)

    out_ref[...] = lax.fori_loop(0, chips - 1, gather, acc)


def body(n, queries, kv_cache, lengths, out_weight, outlier_values, outlier_columns, outlier_counts):
    rows, width = queries.shape
    hl = width // HD
    nr = hl * rows
    positions = kv_cache.shape[2]
    cols = out_weight.shape[1] // n
    omax = outlier_values.shape[1]
    chips = n // 2
    g = n // KVH
    dma = pltpu.SemaphoreType.DMA
    out = pl.pallas_call(
        functools.partial(kernel, n),
        out_shape=jax.ShapeDtypeStruct((rows, cols), F32),
        in_specs=[pl.BlockSpec(memory_space=pl.ANY)] * 7,
        out_specs=pl.BlockSpec(memory_space=pltpu.VMEM),
        scratch_shapes=[
            pltpu.SMEM(lengths.shape, jnp.int32),
            pltpu.SMEM((omax, hl), jnp.int32),
            pltpu.SMEM(outlier_counts.shape, jnp.int32),
            pltpu.VMEM((chips, rows, width), BF16),
            pltpu.VMEM((2, 2, rows, positions, KVH // 2 * HD), BF16),
            pltpu.VMEM((n, width, cols), BF16),
            pltpu.VMEM(outlier_values.shape, BF16),
            pltpu.VMEM((2, g * nr, rows * positions), F32),
            pltpu.VMEM((chips, nr + STAT, HD), BF16),
            pltpu.VMEM((chips, nr + STAT, HD), BF16),
            pltpu.VMEM((rows, width), BF16),
            pltpu.VMEM((hl * omax, rows, HD), F32),
            pltpu.VMEM((chips, rows, cols), F32),
            pltpu.VMEM((chips, rows, cols), F32),
            pltpu.VMEM((chips, rows, cols), BF16),
            pltpu.VMEM((chips, rows, cols), BF16),
            dma((3,)), dma, dma, dma, dma((chips,)), dma((chips,)), dma((n,)), dma, dma((chips,)), dma((chips,)),
            dma((chips,)), dma((chips,)), dma((chips,)), dma((chips,)),
        ],
        compiler_params=pltpu.CompilerParams(
            collective_id=0, has_side_effects=True, vmem_limit_bytes=60 * 2**20
        ),
    )(queries, kv_cache, out_weight, outlier_values, lengths, outlier_columns.T, outlier_counts)
    return out.astype(BF16)


def solution(mesh):
    placed = (
        P("groups", "tensor"),
        P(None, "groups", "tensor", None),
        P("groups"),
        P("tensor", None),
        P("tensor", None, None, None),
        P("tensor", None),
        P("tensor"),
    )
    return jax.shard_map(
        functools.partial(body, mesh.shape["tensor"]),
        mesh=mesh, in_specs=placed, out_specs=P("groups", "tensor"), check_vma=False,
    )
```

```python
import functools
import math

import jax
import jax.numpy as jnp
from jax import lax
from jax.experimental import pallas as pl
from jax.experimental.pallas import tpu as pltpu
from jax.sharding import PartitionSpec as P

KVH = 8
HD = 128
STAT = 16
MESH = pl.DeviceIdType.MESH
F32 = jnp.float32
BF16 = jnp.bfloat16


def flip(a, b, n):
    out, bit = 0, 1
    while bit < n:
        out = out + ((a // bit + b // bit) % 2) * bit
        bit *= 2
    return out


def kernel(
    n,
    q_hbm, kv_hbm, w_hbm, ov_hbm, len_hbm, col_hbm, cnt_hbm,
    out_ref,
    len_ref, col_ref, cnt_ref, qbuf, kvbuf, wbuf, ovbuf, bias, osend, obuf, abuf, tbuf, psend, precv, sbuf, rbuf,
    small_sem, kv_sem, kvs_sem, kvr_sem, qs_sem, qr_sem, w_sem, ov_sem, os_sem, or_sem, ps_sem, pr_sem, ss_sem, sr_sem,
):
    me = lax.axis_index("tensor")
    core = me % 2
    chip = me // 2
    partner = me + 1 - 2 * core
    chips = n // 2
    half = me // chips
    rows, width = q_hbm.shape
    hl = width // HD
    nr = hl * rows
    g = n // KVH
    kh = KVH // 2
    positions = kv_hbm.shape[2]
    cols = w_hbm.shape[1] // n
    omax = ov_hbm.shape[1]
    jb = cols // HD
    hw = kh * HD
    kvcols = rows * positions

    barrier = pltpu.get_barrier_semaphore()
    for i in range(n - 1, 0, -1):
        pl.semaphore_signal(barrier, inc=1, device_id={"tensor": flip(me, i, n)}, device_id_type=MESH)

    def kv_half(c):
        return kv_hbm.at[:, :, :, pl.ds(pl.multiple_of(c * hw, hw), hw)]

    small = [
        pltpu.make_async_copy(src, dst, small_sem.at[i])
        for i, (src, dst) in enumerate(((len_hbm, len_ref), (col_hbm, col_ref), (cnt_hbm, cnt_ref)))
    ]
    for copy in small:
        copy.start()
    kv_own = pltpu.make_async_copy(kv_half(core), kvbuf.at[0], kv_sem)
    kv_own.start()
    ov_copy = pltpu.make_async_copy(ov_hbm, ovbuf, ov_sem)
    my_slot = me - half * chips

    @pl.when(half == core)
    def _():
        pltpu.make_async_copy(q_hbm, qbuf.at[my_slot], qr_sem.at[my_slot]).start()

    def w_copy(i):
        dest = 2 * flip(chip, chips - 1 - i // 2, chips) + (core + 1 + i % 2) % 2
        return pltpu.make_async_copy(
            w_hbm.at[:, pl.ds(pl.multiple_of(dest * cols, cols), cols)], wbuf.at[i], w_sem.at[i]
        )

    for copy in small:
        copy.wait()

    rowreq = lax.broadcasted_iota(jnp.int32, (g * nr, kvcols), 0) % rows
    colidx = lax.broadcasted_iota(jnp.int32, (1, kvcols), 1)
    colreq = colidx // positions
    limit = jnp.zeros((1, kvcols), jnp.int32)
    for r in range(rows):
        limit = jnp.where(colreq == r, len_ref[r], limit)
    for part in range(2):
        dev = me if part == 0 else partner
        live = (colidx % positions + dev * positions) < limit
        tag = jnp.where(live, colreq, -1)
        bias[part] = jnp.where(rowreq == tag, 0.0, -1e30).astype(F32)

    ov_copy.start()

    @pl.loop(0, n)
    def _(i):
        w_copy(i).start()

    pl.semaphore_wait(barrier, n - 1)

    swap = pltpu.make_async_remote_copy(
        src_ref=kv_half(1 - core), dst_ref=kvbuf.at[1], send_sem=kvs_sem, recv_sem=kvr_sem,
        device_id={"tensor": partner}, device_id_type=MESH,
    )
    swap.start()

    def q_send(i):
        p = flip(chip, chips - 1 - i, chips)
        target = 2 * p + half
        return target, pltpu.make_async_remote_copy(
            src_ref=q_hbm, dst_ref=qbuf.at[my_slot], send_sem=qs_sem.at[i], recv_sem=qr_sem.at[my_slot],
            device_id={"tensor": target}, device_id_type=MESH,
        )

    @pl.loop(0, chips)
    def _(i):
        target, copy = q_send(i)

        @pl.when(target != me)
        def _():
            copy.start()

    kv_own.wait()
    swap.wait()

    eye = lax.broadcasted_iota(jnp.int32, (g * nr, HD), 0) == lax.broadcasted_iota(jnp.int32, (g * nr, HD), 1)
    stat_row = lax.broadcasted_iota(jnp.int32, (STAT, HD), 0)

    def to_row(column):
        return jnp.sum(jnp.where(eye, column, 0.0), axis=0, keepdims=True)

    def o_send(j):
        target = core * chips + j
        return target, pltpu.make_async_remote_copy(
            src_ref=osend.at[j], dst_ref=obuf.at[chip], send_sem=os_sem.at[j], recv_sem=or_sem.at[chip],
            device_id={"tensor": target}, device_id_type=MESH,
        )

    def o_local(j):
        return pltpu.make_async_copy(osend.at[j], obuf.at[chip], or_sem.at[chip])

    upper = chip // (chips // 2)
    for step in range(kh):
        kl = step + upper * (kh - 1 - 2 * step)
        lanes = pl.ds(pl.multiple_of(kl * HD, HD), HD)
        pieces = []
        for dl in range(g):
            slot = kl * g + dl
            pltpu.make_async_copy(qbuf.at[slot], qbuf.at[slot], qr_sem.at[slot]).wait()
            got = qbuf[slot].astype(F32)
            pieces += [got[:, h * HD:(h + 1) * HD] for h in range(hl)]
        q = jnp.concatenate(pieces, axis=0).astype(BF16)
        scores, values = [], []
        for part in range(2):
            keys = kvbuf[part, 0, :, :, lanes].reshape(kvcols, HD)
            values.append(kvbuf[part, 1, :, :, lanes].reshape(kvcols, HD))
            s = lax.dot_general(q, keys, (((1,), (1,)), ((), ())), preferred_element_type=F32)
            scores.append(s * (1.0 / math.sqrt(HD)) + bias[part])
        peak = jnp.maximum(
            jnp.max(scores[0], axis=-1, keepdims=True), jnp.max(scores[1], axis=-1, keepdims=True)
        )
        peak = jnp.maximum(peak, -(2.0**66)).astype(BF16).astype(F32)
        total = jnp.zeros((g * nr, 1), F32)
        o = jnp.zeros((g * nr, HD), F32)
        for part in range(2):
            raised = jnp.exp(scores[part] - peak)
            total = total + jnp.sum(raised, axis=-1, keepdims=True)
            o = o + jnp.dot(raised.astype(BF16), values[part], preferred_element_type=F32)
        total_row = to_row(total)
        total_hi = total_row.astype(BF16).astype(F32)
        stats = jnp.where(
            stat_row == 0, to_row(peak), jnp.where(stat_row == 1, total_hi, total_row - total_hi)
        ).astype(BF16)
        o = o.astype(BF16)
        for dl in range(g):
            slot = kl * g + dl
            osend[slot, :nr, :] = o[dl * nr:(dl + 1) * nr]
            osend[slot, nr:, :] = stats
            target, copy = o_send(slot)

            @pl.when(target != me)
            def _():
                copy.start()

            @pl.when(target == me)
            def _():
                o_local(slot).start()

    for p in range(chips):
        pltpu.make_async_copy(obuf.at[p], obuf.at[p], or_sem.at[p]).wait()
    peaks, totals = [], []
    for p in range(chips):
        st = obuf[p, nr:, :].astype(F32)
        peaks.append(st[0:1])
        totals.append(st[1:2] + st[2:3])
    peak = functools.reduce(jnp.maximum, peaks)
    shares = [jnp.exp(m - peak) for m in peaks]
    total = sum(s * t for s, t in zip(shares, totals))
    first = (me % g) * nr
    mine = (
        lax.broadcasted_iota(jnp.int32, (nr, HD), 0) + first
        == lax.broadcasted_iota(jnp.int32, (nr, HD), 1)
    )
    attended = jnp.zeros((nr, HD), F32)
    for p in range(chips):
        share = jnp.sum(jnp.where(mine, shares[p] / total, 0.0), axis=1, keepdims=True)
        attended = attended + share * obuf[p, :nr, :].astype(F32)
    a = jnp.concatenate([attended[h * rows:(h + 1) * rows] for h in range(hl)], axis=1).astype(BF16)
    abuf[...] = a

    ov_copy.wait()
    for h in range(hl):
        for o in range(omax):
            tbuf[h * omax + o] = jnp.dot(
                a[:, h * HD:(h + 1) * HD], ovbuf[h, o], preferred_element_type=F32
            )

    def block(i):
        dest = 2 * flip(chip, chips - 1 - i // 2, chips) + (core + 1 + i % 2) % 2
        w_copy(i).wait()
        part = jnp.dot(abuf[...], wbuf[i], preferred_element_type=F32)
        sums = [part[:, j * HD:(j + 1) * HD] for j in range(jb)]
        for h in range(hl):
            for o in range(omax):
                col = jnp.where(o < cnt_ref[h], col_ref[o, h] - dest * jb, -1)
                colv = jnp.full((rows, HD), col, jnp.int32)
                term = tbuf[h * omax + o]
                sums = [s + jnp.where(colv == j, term, 0.0) for j, s in enumerate(sums)]
        return jnp.concatenate(sums, axis=1)

    def p_send(i):
        return pltpu.make_async_remote_copy(
            src_ref=psend.at[i], dst_ref=precv.at[i], send_sem=ps_sem.at[i], recv_sem=pr_sem.at[i],
            device_id={"tensor": partner}, device_id_type=MESH,
        )

    def s_send(i):
        return pltpu.make_async_remote_copy(
            src_ref=sbuf.at[i], dst_ref=rbuf.at[i], send_sem=ss_sem.at[i], recv_sem=sr_sem.at[i],
            device_id={"tensor": 2 * flip(chip, chips - 1 - i, chips) + core}, device_id_type=MESH,
        )

    psend[0] = block(0)
    p_send(0).start()

    @pl.loop(0, chips - 1, unroll=True)
    def _(i):
        psend[i + 1] = block(2 * i + 2)
        p_send(i + 1).start()
        sums = block(2 * i + 1)
        p_send(i).wait_recv()
        sbuf[i] = (sums + precv[i]).astype(sbuf.dtype)
        s_send(i).start()

    acc = block(n - 1)
    p_send(chips - 1).wait_recv()
    acc = acc + precv[chips - 1]

    @pl.loop(0, chips)
    def _(i):
        target, copy = q_send(i)

        @pl.when(target != me)
        def _():
            copy.wait_send()

        target2, copy2 = o_send(i)

        @pl.when(target2 != me)
        def _():
            copy2.wait_send()

        p_send(i).wait_send()

    def gather(i, acc):
        s_send(i).wait()
        return acc + rbuf[i].astype(F32)

    out_ref[...] = lax.fori_loop(0, chips - 1, gather, acc)


def body(n, queries, kv_cache, lengths, out_weight, outlier_values, outlier_columns, outlier_counts):
    rows, width = queries.shape
    hl = width // HD
    nr = hl * rows
    positions = kv_cache.shape[2]
    cols = out_weight.shape[1] // n
    omax = outlier_values.shape[1]
    chips = n // 2
    g = n // KVH
    dma = pltpu.SemaphoreType.DMA
    out = pl.pallas_call(
        functools.partial(kernel, n),
        out_shape=jax.ShapeDtypeStruct((rows, cols), F32),
        in_specs=[pl.BlockSpec(memory_space=pl.ANY)] * 7,
        out_specs=pl.BlockSpec(memory_space=pltpu.VMEM),
        scratch_shapes=[
            pltpu.SMEM(lengths.shape, jnp.int32),
            pltpu.SMEM((omax, hl), jnp.int32),
            pltpu.SMEM(outlier_counts.shape, jnp.int32),
            pltpu.VMEM((chips, rows, width), BF16),
            pltpu.VMEM((2, 2, rows, positions, KVH // 2 * HD), BF16),
            pltpu.VMEM((n, width, cols), BF16),
            pltpu.VMEM(outlier_values.shape, BF16),
            pltpu.VMEM((2, g * nr, rows * positions), F32),
            pltpu.VMEM((chips, nr + STAT, HD), BF16),
            pltpu.VMEM((chips, nr + STAT, HD), BF16),
            pltpu.VMEM((rows, width), BF16),
            pltpu.VMEM((hl * omax, rows, HD), F32),
            pltpu.VMEM((chips, rows, cols), F32),
            pltpu.VMEM((chips, rows, cols), F32),
            pltpu.VMEM((chips, rows, cols), BF16),
            pltpu.VMEM((chips, rows, cols), BF16),
            dma((3,)), dma, dma, dma, dma((chips,)), dma((chips,)), dma((n,)), dma, dma((chips,)), dma((chips,)),
            dma((chips,)), dma((chips,)), dma((chips,)), dma((chips,)),
        ],
        compiler_params=pltpu.CompilerParams(
            collective_id=0, has_side_effects=True, vmem_limit_bytes=60 * 2**20
        ),
    )(queries, kv_cache, out_weight, outlier_values, lengths, outlier_columns.T, outlier_counts)
    return out.astype(BF16)


def solution(mesh):
    placed = (
        P("groups", "tensor"),
        P(None, "groups", "tensor", None),
        P("groups"),
        P("tensor", None),
        P("tensor", None, None, None),
        P("tensor", None),
        P("tensor"),
    )
    return jax.shard_map(
        functools.partial(body, mesh.shape["tensor"]),
        mesh=mesh, in_specs=placed, out_specs=P("groups", "tensor"), check_vma=False,
    )
```
